32 devices in a mesh: gx: 4 (over z), gy: 2 (over x), gz: 4 (over y, core).
Axes of the slice: x: 2, y: 2, z: 4, core: 2. Of those that a mesh axis runs over, the one named last changes fastest.
Arguments:
- loads: float32 [4, 2, 4, 1024, 128], P('gx', 'gy', 'gz'), may hold values from -12 to 12
- start: float32 [4, 2, 4, 1024, 128], P('gx', 'gy', 'gz'), may hold values from -6 to 6
- schur: float32 [4, 2, 4, 1024, 1024], P('gx', 'gy', 'gz'), may hold values from -2 to 8
- inv_local: float32 [4, 2, 4, 1024, 1024], P('gx', 'gy', 'gz'), may hold values from -1 to 3
- basis: float32 [4, 2, 4, 1024, 128], P('gx', 'gy', 'gz'), may hold values from -0.1875 to 0.1875
- coarse_inv: float32 [4096, 4096], P(('gx', 'gy')), may hold values from -0.01 to 0.07
- face_index: int32 [4, 2, 4, 6, 160], P('gx', 'gy', 'gz'), may hold values from 0 to 1023, as said below
- multiplicity: int32 [4, 2, 4, 1024], P('gx', 'gy', 'gz'), may hold values from 1 to 2, as said below
- primal_map: int32 [4, 2, 4, 128], P('gx', 'gy', 'gz'), may hold values from 0 to 4095, all different within a row
Outputs:
- solution: float32 [4, 2, 4, 1024, 128], P('gx', 'gy', 'gz')
- residual: float32 [4, 2, 4, 1024, 128], P('gx', 'gy', 'gz')
The draws below stay inside these ranges and needn't reach their ends.
Inputs may be any that keep to these rules, and one draw needn't show every extreme that they name: face_index[x, y, z, 2a + s] lists 160 distinct interface slots of subdomain (x, y, z) on its face toward the lower (s = 0) or higher (s = 1) neighbour along grid direction a; the six lists of one subdomain are disjoint. `multiplicity`: 1, plus 1 on slots listed in a face whose neighbouring subdomain lies inside the grid. `primal_map`: each subdomain lists 128 distinct primal unknowns, and every primal unknown is listed by some subdomain.
All inputs are finite; a program needn't handle non-finite values.
Results may differ from the reference program's by a relative error of at most 0.00012.
Values sent between devices are 32-bit elements; how exact they have to be, the bound alone decides.
A program may use at most 64 MiB of HBM per device.

```python
import math
import jax
import jax.numpy as jnp
from jax import lax

NI = 1024
FACE = 160
NPL = 128
NPRIM = 4096
L = 128
ITERS = 2
SX = 4
SY = 2
SZ = 4


def stiffness(key):
    return jnp.exp(jax.random.uniform(jax.random.fold_in(key, 7), (SX, SY, SZ), jnp.float32, math.log(0.5), math.log(4.0)))


def symmetric_noise(key, order, level):
    normal_draw = jax.random.normal(key, (order, order), jnp.float32)
    return (normal_draw + normal_draw.T) * (level / math.sqrt(2.0 * order))


def local_matrices(key, label, low, high, level):
    subdomains = SX * SY * SZ
    subkeys = jax.random.split(jax.random.fold_in(key, label), subdomains)

    def single(subkey):
        first_key, second_key = jax.random.split(subkey)
        diagonal = jax.random.uniform(first_key, (NI,), jnp.float32, low, high)
        return jnp.diag(diagonal) + symmetric_noise(second_key, NI, level)
    return lax.map(single, subkeys)


def draw_schur(key, part):
    matrices = local_matrices(key, 21, 0.75, 1.5, 0.3)
    scaled = matrices * stiffness(key).reshape(-1, 1, 1)
    return scaled.reshape(SX, SY, SZ, NI, NI)


def draw_inv_local(key, part):
    matrices = local_matrices(key, 22, 0.6, 1.2, 0.2)
    scaled = matrices / stiffness(key).reshape(-1, 1, 1)
    return scaled.reshape(SX, SY, SZ, NI, NI)


def draw_coarse_inv(key, part):
    first_key, second_key = jax.random.split(jax.random.fold_in(key, 23))
    diagonal = jax.random.uniform(first_key, (NPRIM,), jnp.float32, 0.03, 0.06)
    return jnp.diag(diagonal) + symmetric_noise(second_key, NPRIM, 0.01)


def face_lists(key):
    subdomains = SX * SY * SZ
    subkeys = jax.random.split(jax.random.fold_in(key, 11), subdomains)
    orders = jax.vmap(lambda subkey: jax.random.permutation(subkey, NI))(subkeys)
    return orders[:, :6 * FACE].reshape(SX, SY, SZ, 6, FACE).astype(jnp.int32)


def draw_face_index(key, part):
    return face_lists(key)


def draw_multiplicity(key, part):
    lists = face_lists(key)
    subdomains = SX * SY * SZ
    first = jnp.broadcast_to(jnp.arange(SX).reshape(SX, 1, 1), (SX, SY, SZ))
    second = jnp.broadcast_to(jnp.arange(SY).reshape(1, SY, 1), (SX, SY, SZ))
    third = jnp.broadcast_to(jnp.arange(SZ).reshape(1, 1, SZ), (SX, SY, SZ))
    exists = jnp.stack([first > 0, first < SX - 1, second > 0, second < SY - 1, third > 0, third < SZ - 1], axis=-1).astype(jnp.int32)
    flags = jnp.broadcast_to(exists[..., None], lists.shape)
    base = jnp.ones((subdomains, NI), jnp.int32)
    counted = jax.vmap(lambda rows, where, extra: rows.at[where].add(extra))(base, lists.reshape(subdomains, -1), flags.reshape(subdomains, -1))
    return counted.reshape(SX, SY, SZ, NI)


def shard_levels(key, extent, pieces, smallest, high):
    gain = 1.0
    for position, shards_of in pieces:
        draws = jax.random.uniform(jax.random.fold_in(jax.random.fold_in(key, 6), position), (shards_of,), jnp.float32, smallest / len(pieces), high / len(pieces))
        gain = gain * jnp.repeat(jnp.exp(draws), extent[position] // shards_of).reshape((-1,) + (1,) * (len(extent) - 1 - position))
    return gain


def picks_of(stream_key, rows, amount, top, lift):
    order = jax.random.permutation(jax.random.fold_in(stream_key, 1), amount)
    pull = order
    for power in range(3):
        pull = pull * pull // amount
    pull = pull * lift // amount
    tickets = jax.random.randint(jax.random.fold_in(stream_key, 2), (rows, amount), 0, 4096) + pull
    holders = jax.random.permutation(jax.random.fold_in(stream_key, 3), rows)[jnp.arange(amount) % rows]
    tickets = jnp.where(jnp.arange(rows)[:, None] == holders[None, :], 1 << 14, tickets)
    priority = tickets * amount + jnp.arange(amount)
    return lax.top_k(priority.astype(jnp.int32), top)[1].astype(jnp.int32)


def bell_draw(stream_key, shape, spread, reach, shards=(), kind=jnp.bfloat16):
    values = jax.random.normal(stream_key, shape, jnp.float32) * spread
    if len(shards) > 0:
        values = shard_levels(stream_key, shape, shards, -0.22, 0.18) * values
    return jnp.clip(values, min=-reach, max=reach).astype(kind)


def setup_inputs(seed: int = 0) -> dict:
    key_of = jax.random.split(jax.random.key(seed), 10)
    loads = bell_draw(key_of[0], (SX, SY, SZ, NI, L), 2.0, 12.0, ((0, 4), (1, 2), (2, 4)), jnp.float32)
    start = bell_draw(key_of[1], (SX, SY, SZ, NI, L), 1.0, 6.0, ((0, 4), (1, 2), (2, 4)), jnp.float32)
    schur = draw_schur(jax.random.fold_in(key_of[9], 71), 0)
    inv_local = draw_inv_local(jax.random.fold_in(key_of[9], 71), 0)
    basis = bell_draw(key_of[4], (SX, SY, SZ, NI, NPL), NI ** -0.5, 0.1875, ((0, 4), (1, 2), (2, 4)), jnp.float32)
    coarse_inv = draw_coarse_inv(jax.random.fold_in(key_of[9], 71), 0)
    face_index = draw_face_index(jax.random.fold_in(key_of[9], 71), 0)
    multiplicity = draw_multiplicity(jax.random.fold_in(key_of[9], 71), 0)
    primal_map = picks_of(key_of[8], SX * SY * SZ, NPRIM, NPL, 0).reshape((SX, SY, SZ, NPL))
    return dict(loads=loads, start=start, schur=schur, inv_local=inv_local, basis=basis, coarse_inv=coarse_inv, face_index=face_index, multiplicity=multiplicity, primal_map=primal_map)


damping = 0.6


def from_lower(array, axis):
    length = array.shape[axis]
    widths = [(0, 0)] * array.ndim
    widths[axis] = (1, 0)
    return lax.slice_in_dim(jnp.pad(array, widths), 0, length, axis=axis)


def from_upper(array, axis):
    length = array.shape[axis]
    widths = [(0, 0)] * array.ndim
    widths[axis] = (0, 1)
    return lax.slice_in_dim(jnp.pad(array, widths), 1, length + 1, axis=axis)


def interface_sum(field, face_index):
    grid = field.shape[:3]
    unknowns = field.shape[3]
    load_cases = field.shape[4]
    flat = field.reshape(-1, unknowns, load_cases)
    slots = face_index.reshape(flat.shape[0], -1)
    gathered = jax.vmap(lambda rows, where: rows[where])(flat, slots)
    face_values = gathered.reshape(grid + (6, face_index.shape[4], load_cases))
    received = []
    for axis in range(3):
        received.append(from_lower(face_values[:, :, :, 2 * axis + 1], axis))
        received.append(from_upper(face_values[:, :, :, 2 * axis], axis))
    arrived = jnp.stack(received, axis=3).reshape(flat.shape[0], -1, load_cases)
    summed = jax.vmap(lambda rows, where, extra: rows.at[where].add(extra))(flat, slots, arrived)
    return summed.reshape(field.shape)


def batched(matrices, vectors):
    return jnp.einsum('pij,pjl->pil', matrices, vectors, precision=lax.Precision.HIGHEST)


def reference(loads, start, schur, inv_local, basis, coarse_inv, face_index, multiplicity, primal_map):
    subdomains = loads.shape[0] * loads.shape[1] * loads.shape[2]
    unknowns = loads.shape[3]
    load_cases = loads.shape[4]
    flat_schur = schur.reshape(subdomains, unknowns, unknowns)
    flat_inverse = inv_local.reshape(subdomains, unknowns, unknowns)
    flat_basis = basis.reshape(subdomains, unknowns, -1)
    weight = 1.0 / multiplicity.astype(jnp.float32)[..., None]
    primal_ids = primal_map.reshape(subdomains, -1)
    solution = start
    residual = start
    for iteration in range(ITERS):
        product = batched(flat_schur, solution.reshape(subdomains, unknowns, load_cases)).reshape(loads.shape)
        residual = loads - interface_sum(product, face_index)
        weighted = (weight * residual).reshape(subdomains, unknowns, load_cases)
        local = batched(flat_inverse, weighted)
        terms = jnp.einsum('pin,pil->pnl', flat_basis, weighted, precision=lax.Precision.HIGHEST)
        coarse_load = jnp.zeros((coarse_inv.shape[0], load_cases), jnp.float32).at[primal_ids.reshape(-1)].add(terms.reshape(-1, load_cases))
        coarse_sol = jnp.dot(coarse_inv, coarse_load, precision=lax.Precision.HIGHEST, preferred_element_type=jnp.float32)
        correction = batched(flat_basis, coarse_sol[primal_ids])
        update = interface_sum(weight * (local + correction).reshape(loads.shape), face_index)
        solution = solution + damping * update
    return solution, residual
```

```python
import functools
import itertools

import jax
import jax.numpy as jnp
from jax import lax
from jax.experimental import pallas as pl
from jax.experimental.pallas import tpu as pltpu
from jax.sharding import PartitionSpec as P

ITERS = 2
damping = 0.6
MESH = pl.DeviceIdType.MESH
AXES = ("gx", "gy", "gz")


class Grid:
    def __init__(self, sizes):
        self.sizes = sizes
        gx, gy, gz = sizes
        self.lo = 2 if gz % 2 == 0 else 1
        self.hi = gz // self.lo
        self.stages = (gx, gy, self.hi, self.lo)
        self.count = gx * gy * gz
        self.c = tuple(lax.axis_index(a) for a in AXES)
        self.place = (self.c[0], self.c[1], self.c[2] // self.lo, self.c[2] % self.lo)

    def linear(self, place):
        x, y, h, l = place
        return (x * self.sizes[1] + y) * self.sizes[2] + h * self.lo + l

    def device(self, place):
        x, y, h, l = place
        return (x, y, h * self.lo + l)

    def barrier(self):
        semaphore = pltpu.get_barrier_semaphore()
        total = 0
        for axis in range(3):
            for delta in range(1, self.sizes[axis]):
                target = list(self.c)
                target[axis] = (self.c[axis] + delta) % self.sizes[axis]
                pl.semaphore_signal(
                    semaphore, inc=1, device_id=tuple(target), device_id_type=MESH
                )
                total += 1
        if total:
            pl.semaphore_wait(semaphore, total)


class Gather:
    def __init__(self, grid, buffer, rows, send, recv):
        self.grid, self.buffer, self.rows = grid, buffer, rows
        self.send, self.recv = send, recv
        self.sent = []

    def block(self, offset):
        g = self.grid
        place = tuple((c + n - d) % n for c, d, n in zip(g.place, offset, g.stages))
        return self.buffer.at[pl.ds(g.linear(place) * self.rows, self.rows)]

    def number(self, offset):
        value = 0
        for d, n in zip(offset, self.grid.stages):
            value = value * n + d
        return value

    def copy(self, offset, stage, delta):
        g = self.grid
        arrived = list(offset)
        arrived[stage] = delta
        place = list(g.place)
        place[stage] = (g.place[stage] + delta) % g.stages[stage]
        block = self.block(offset)
        k = self.number(arrived)
        return pltpu.make_async_remote_copy(
            src_ref=block, dst_ref=block, send_sem=self.send.at[k], recv_sem=self.recv.at[k],
            device_id=g.device(place), device_id_type=MESH,
        )

    def forward(self, offset, first):
        for stage in range(first, 4):
            for delta in range(1, self.grid.stages[stage]):
                c = self.copy(offset, stage, delta)
                c.start()
                self.sent.append(c)

    def start(self):
        self.forward((0, 0, 0, 0), 0)

    def finish(self):
        g = self.grid
        for stage in range(4):
            earlier = [range(n) for n in g.stages[:stage]]
            for head in itertools.product(*earlier):
                for delta in range(1, g.stages[stage]):
                    arrived = tuple(head) + (delta,) + (0,) * (3 - stage)
                    block = self.block(arrived)
                    k = self.number(arrived)
                    pltpu.make_async_remote_copy(
                        src_ref=block, dst_ref=block, send_sem=self.send.at[k],
                        recv_sem=self.recv.at[k], device_id=g.c, device_id_type=MESH,
                    ).wait_recv()
                    self.forward(arrived, stage + 1)

    def drain(self):
        for c in self.sent:
            c.wait_send()


def map_kernel(sizes, own_ref, all_ref, send, recv):
    grid = Grid(sizes)
    rows = own_ref.shape[0]
    all_ref[pl.ds(grid.linear(grid.place) * rows, rows), :] = own_ref[...]
    grid.barrier()
    gather = Gather(grid, all_ref, rows, send, recv)
    gather.start()
    gather.finish()
    gather.drain()


def split(value):
    high = value.astype(jnp.bfloat16)
    low = (value - high.astype(jnp.float32)).astype(jnp.bfloat16)
    return high, low


def tile_of(total, want):
    while total % want:
        want //= 2
    return want


def split_rows(source, high, low):
    rows = source.shape[0]
    tile = tile_of(rows, 64)

    def step(i, carry):
        r = pl.ds(pl.multiple_of(i * tile, tile), tile)
        h, l = split(source[r, :])
        high[r, :] = h
        low[r, :] = l
        return carry

    lax.fori_loop(0, rows // tile, step, 0)


def split_beside(source, both):
    rows, width = source.shape
    tile = tile_of(rows, 128)

    def step(i, carry):
        r = pl.ds(pl.multiple_of(i * tile, tile), tile)
        h, l = split(source[r, :])
        both[r, 0:width] = h
        both[r, width : 2 * width] = l
        return carry

    lax.fori_loop(0, rows // tile, step, 0)


def product(high, low, both):
    width = both.shape[1] // 2
    wide = jnp.dot(high, both[...], preferred_element_type=jnp.float32)
    thin = jnp.dot(low, both[:, 0:width], preferred_element_type=jnp.float32)
    return wide[:, 0:width] + wide[:, width:] + thin


def by_rows(rows, want, function):
    tile = tile_of(rows, want)

    def step(i, carry):
        function(pl.ds(pl.multiple_of(i * tile, tile), tile))
        return carry

    lax.fori_loop(0, rows // tile, step, 0)


def take_rows(target, source, index, count, base=0):
    unroll = tile_of(count, 16)

    def step(i, carry):
        first = pl.multiple_of(i * unroll, unroll)
        for j in range(unroll):
            row = index[base + first + j]
            target[pl.ds(first + j, 1), :] = source[pl.ds(row, 1), :]
        return carry

    lax.fori_loop(0, count // unroll, step, 0)


def main_kernel(
    sizes, face,
    slots, places, own_map, all_map,
    loads, start, basis, basis_t, weight, schur, inverse, coarse_t,
    solution, residual,
    full, s_high, s_low, b_high, b_low, m_high, m_low, t_high, t_low,
    c_high, c_low, picked, field, local, moved, both, term_both, sol_both, coarse_rows,
    faces, arrived, term_all, sol_all,
    load_sem, face_send, face_recv, term_send, term_recv, sol_send, sol_recv,
):
    grid = Grid(sizes)
    unknowns, cases = start.shape
    primal = basis.shape[1]
    own = coarse_t.shape[1]
    load_s = pltpu.make_async_copy(schur, full, load_sem.at[0])
    load_b = pltpu.make_async_copy(inverse, full, load_sem.at[1])
    load_s.start()
    for landing in arrived:
        landing[...] = jnp.zeros_like(landing)
    grid.barrier()
    split_rows(basis, m_high, m_low)
    split_rows(basis_t, t_high, t_low)
    solution[...] = start[...]
    sent = []

    def face_copy(turn, d):
        axis, side = d // 2, d % 2
        target = list(grid.c)
        target[axis] = grid.c[axis] + (1 if side else -1)
        return pltpu.make_async_remote_copy(
            src_ref=faces.at[turn, pl.ds(d * face, face)],
            dst_ref=arrived[turn].at[pl.ds((d ^ 1) * face, face)],
            send_sem=face_send.at[turn, d],
            recv_sem=face_recv.at[turn, d ^ 1],
            device_id=tuple(target), device_id_type=MESH,
        )

    def exists(d):
        axis, side = d // 2, d % 2
        return grid.c[axis] < sizes[axis] - 1 if side else grid.c[axis] > 0

    def exchange_start(turn):
        for d in range(6):
            take_rows(faces.at[turn, pl.ds(d * face, face)], field, slots, face, d * face)

            @pl.when(exists(d))
            def _():
                face_copy(turn, d).start()

    def exchange_finish(turn):
        for d in range(6):

            @pl.when(exists(d))
            def _():
                block = arrived[turn].at[pl.ds(d * face, face)]
                pltpu.make_async_remote_copy(
                    src_ref=block, dst_ref=block, send_sem=face_send.at[turn, d],
                    recv_sem=face_recv.at[turn, d], device_id=grid.c, device_id_type=MESH,
                ).wait_recv()

        take_rows(moved, arrived[turn], places, unknowns)

    def exchange_drain(turn):
        for d in range(6):

            @pl.when(exists(d))
            def _():
                face_copy(turn, d).wait_send()

    gathers = []
    for iteration in range(ITERS):
        turn = 2 * iteration
        split_beside(solution, both)
        if iteration == 0:
            load_s.wait()
            split_rows(full, s_high, s_low)
            load_b.start()

        def stiff(r):
            field[r, :] = product(s_high[r, :], s_low[r, :], both)

        by_rows(unknowns, 256, stiff)
        exchange_start(turn)
        if iteration == 0:
            load_b.wait()
            split_rows(full, b_high, b_low)

            def pick(p, carry):
                take_rows(picked, coarse_t, all_map, primal, p * primal)
                h, l = split(picked[...].T)
                k = pl.ds(pl.multiple_of(p * primal, primal), primal)
                c_high[:, k] = h
                c_low[:, k] = l
                return carry

            lax.fori_loop(0, grid.count, pick, 0)
        exchange_finish(turn)

        def settle(r):
            value = loads[r, :] - (field[r, :] + moved[r, :])
            residual[r, :] = value
            scaled = weight[r, :] * value
            h, l = split(scaled)
            both[r, 0:cases] = h
            both[r, cases : 2 * cases] = l

        by_rows(unknowns, 128, settle)
        mine = pl.multiple_of(grid.linear(grid.place) * primal, primal)
        term_all[iteration, pl.ds(mine, primal), :] = product(t_high[...], t_low[...], both)
        terms = Gather(grid, term_all.at[iteration], primal, term_send.at[iteration], term_recv.at[iteration])
        terms.start()
        gathers.append(terms)

        def invert(r):
            local[r, :] = product(b_high[r, :], b_low[r, :], both)

        by_rows(unknowns, 256, invert)
        terms.finish()
        mine = pl.multiple_of(grid.linear(grid.place) * own, own)
        coarse_tile = term_both.shape[0]
        sol_all[iteration][pl.ds(mine, own), :] = jnp.zeros((own, cases), jnp.float32)

        def coarse(i, carry):
            k = pl.ds(pl.multiple_of(i * coarse_tile, coarse_tile), coarse_tile)
            split_beside(term_all.at[iteration, k], term_both)
            sol_all[iteration][pl.ds(mine, own), :] += product(c_high[:, k], c_low[:, k], term_both)
            return carry

        lax.fori_loop(0, grid.count * primal // coarse_tile, coarse, 0)
        sols = Gather(grid, sol_all[iteration], own, sol_send.at[iteration], sol_recv.at[iteration])
        sols.start()
        sols.finish()
        gathers.append(sols)
        take_rows(coarse_rows, sol_all[iteration], own_map, primal)
        split_beside(coarse_rows, sol_both)

        def correct(r):
            field[r, :] = weight[r, :] * (local[r, :] + product(m_high[r, :], m_low[r, :], sol_both))

        by_rows(unknowns, 256, correct)
        exchange_start(turn + 1)
        exchange_finish(turn + 1)

        def advance(r):
            solution[r, :] = solution[r, :] + damping * (field[r, :] + moved[r, :])

        by_rows(unknowns, 128, advance)
    for turn in range(2 * ITERS):
        exchange_drain(turn)
    for gather in gathers:
        gather.drain()


def places_of(slots, unknowns):
    count = slots.shape[0]
    hit = slots[:, None] == jnp.arange(unknowns, dtype=jnp.int32)[None, :]
    position = jnp.arange(count, dtype=jnp.int32)[:, None] - count
    return jnp.sum(jnp.where(hit, position, 0), axis=0) + count


def body(sizes, loads, start, schur, inv_local, basis, coarse_inv, face_index, multiplicity, primal_map):
    unknowns, cases = loads.shape[3:]
    face = face_index.shape[4]
    primal = basis.shape[4]
    count = sizes[0] * sizes[1] * sizes[2]
    total = coarse_inv.shape[1]
    own = coarse_inv.shape[0] // sizes[2]
    slots = face_index.reshape(-1)
    places = places_of(slots, unknowns)
    own_map = primal_map.reshape(-1)
    vmem = pl.BlockSpec(memory_space=pltpu.VMEM)
    smem = pl.BlockSpec(memory_space=pltpu.SMEM)
    anywhere = pl.BlockSpec(memory_space=pl.ANY)
    dma = pltpu.SemaphoreType.DMA
    maps = pl.pallas_call(
        functools.partial(map_kernel, sizes),
        out_shape=jax.ShapeDtypeStruct((count * 8, primal), jnp.int32),
        in_specs=[vmem],
        out_specs=vmem,
        scratch_shapes=[dma((count,)), dma((count,))],
        compiler_params=pltpu.CompilerParams(collective_id=0, has_side_effects=True),
    )(jnp.broadcast_to(own_map[None, :], (8, primal)))
    all_map = maps.reshape(count, 8, primal)[:, 0, :].reshape(-1)
    own_rows = lax.dynamic_slice_in_dim(coarse_inv, lax.axis_index("gz") * own, own, 0)
    weight = jnp.broadcast_to(
        1.0 / multiplicity.reshape(unknowns, 1).astype(jnp.float32), (unknowns, cases)
    )
    modes = basis.reshape(unknowns, primal)
    f32, bf16 = jnp.float32, jnp.bfloat16
    turns = 2 * ITERS
    coarse_tile = tile_of(count * primal, 1024)
    vec = pltpu.VMEM((unknowns, cases), f32)
    out = jax.ShapeDtypeStruct((unknowns, cases), f32)
    solution, residual = pl.pallas_call(
        functools.partial(main_kernel, sizes, face),
        out_shape=(out, out),
        in_specs=[smem] * 4 + [vmem] * 5 + [anywhere] * 2 + [vmem],
        out_specs=(vmem, vmem),
        scratch_shapes=[
            pltpu.VMEM((unknowns, unknowns), f32),
            pltpu.VMEM((unknowns, unknowns), bf16),
            pltpu.VMEM((unknowns, unknowns), bf16),
            pltpu.VMEM((unknowns, unknowns), bf16),
            pltpu.VMEM((unknowns, unknowns), bf16),
            pltpu.VMEM((unknowns, primal), bf16),
            pltpu.VMEM((unknowns, primal), bf16),
            pltpu.VMEM((primal, unknowns), bf16),
            pltpu.VMEM((primal, unknowns), bf16),
            pltpu.VMEM((own, count * primal), bf16),
            pltpu.VMEM((own, count * primal), bf16),
            pltpu.VMEM((primal, own), f32),
            vec, vec, vec,
            pltpu.VMEM((unknowns, 2 * cases), bf16),
            pltpu.VMEM((coarse_tile, 2 * cases), bf16),
            pltpu.VMEM((primal, 2 * cases), bf16),
            pltpu.VMEM((primal, cases), f32),
            pltpu.VMEM((turns, 6 * face, cases), f32),
            [pltpu.VMEM((6 * face + 8, cases), f32) for _ in range(turns)],
            pltpu.VMEM((ITERS, count * primal, cases), f32),
            [pltpu.VMEM((total, cases), f32) for _ in range(ITERS)],
            dma((2,)),
            dma((turns, 6)), dma((turns, 6)),
            dma((ITERS, count)), dma((ITERS, count)),
            dma((ITERS, count)), dma((ITERS, count)),
        ],
        compiler_params=pltpu.CompilerParams(
            collective_id=1, has_side_effects=True, vmem_limit_bytes=67043328
        ),
    )(
        slots, places, own_map, all_map,
        loads.reshape(unknowns, cases), start.reshape(unknowns, cases),
        modes, modes.T, weight,
        schur.reshape(unknowns, unknowns), inv_local.reshape(unknowns, unknowns), own_rows.T,
    )
    return (solution.reshape(loads.shape), residual.reshape(loads.shape))


def solution(mesh):
    sizes = tuple(mesh.shape[a] for a in AXES)
    field = P("gx", "gy", "gz", None, None)
    placed = (field,) * 5 + (P(("gx", "gy"), None), field, P("gx", "gy", "gz", None), P("gx", "gy", "gz", None))
    return jax.shard_map(
        functools.partial(body, sizes),
        mesh=mesh,
        in_specs=placed,
        out_specs=(field, field),
        check_vma=False,
    )
```

```python
import functools
import itertools

import jax
import jax.numpy as jnp
from jax import lax
from jax.experimental import pallas as pl
from jax.experimental.pallas import tpu as pltpu
from jax.sharding import PartitionSpec as P

ITERS = 2
damping = 0.6
MESH = pl.DeviceIdType.MESH
AXES = ("gx", "gy", "gz")


class Grid:
    def __init__(self, sizes):
        self.sizes = sizes
        gx, gy, gz = sizes
        self.lo = 2 if gz % 2 == 0 else 1
        self.hi = gz // self.lo
        self.stages = (gx, gy, self.hi, self.lo)
        self.count = gx * gy * gz
        self.c = tuple(lax.axis_index(a) for a in AXES)
        self.place = (self.c[0], self.c[1], self.c[2] // self.lo, self.c[2] % self.lo)

    def linear(self, place):
        x, y, h, l = place
        return (x * self.sizes[1] + y) * self.sizes[2] + h * self.lo + l

    def device(self, place):
        x, y, h, l = place
        return (x, y, h * self.lo + l)

    def barrier(self):
        semaphore = pltpu.get_barrier_semaphore()
        total = 0
        for axis in range(3):
            for delta in range(1, self.sizes[axis]):
                target = list(self.c)
                target[axis] = (self.c[axis] + delta) % self.sizes[axis]
                pl.semaphore_signal(
                    semaphore, inc=1, device_id=tuple(target), device_id_type=MESH
                )
                total += 1
        if total:
            pl.semaphore_wait(semaphore, total)


class Gather:
    def __init__(self, grid, buffer, whole, band, order, send, recv):
        self.grid, self.buffer, self.whole, self.band = grid, buffer, whole, band
        self.order, self.send, self.recv = order, send, recv
        self.lengths = tuple(grid.stages[o] for o in order)

    def place(self, offset):
        g = self.grid
        place = list(g.place)
        for o, d in zip(self.order, offset):
            if d:
                place[o] = (g.place[o] + g.stages[o] - d) % g.stages[o]
        return place

    def block(self, offset):
        first = self.grid.linear(self.place(offset)) * self.whole + self.band[0]
        return self.buffer.at[pl.ds(pl.multiple_of(first, 8), self.band[1])]

    def number(self, offset):
        value = 0
        for d, n in zip(offset, self.lengths):
            value = value * n + d
        return value

    def forward(self, offset, first):
        for stage in range(first, 4):
            for delta in range(1, self.lengths[stage]):
                back = [0, 0, 0, 0]
                back[stage] = self.lengths[stage] - delta
                arrived = list(offset)
                arrived[stage] = delta
                k = self.number(arrived)
                block = self.block(offset)
                c = pltpu.make_async_remote_copy(
                    src_ref=block, dst_ref=block, send_sem=self.send,
                    recv_sem=self.recv.at[k], device_id=self.grid.device(self.place(back)),
                    device_id_type=MESH,
                )
                c.start()

    def start(self):
        self.forward((0, 0, 0, 0), 0)

    def finish(self, stage):
        for head in itertools.product(*[range(n) for n in self.lengths[:stage]]):
            for delta in range(1, self.lengths[stage]):
                arrived = tuple(head) + (delta,) + (0,) * (3 - stage)
                block = self.block(arrived)
                k = self.number(arrived)
                pltpu.make_async_remote_copy(
                    src_ref=block, dst_ref=block, send_sem=self.send,
                    recv_sem=self.recv.at[k], device_id=self.grid.c, device_id_type=MESH,
                ).wait_recv()
                self.forward(arrived, stage + 1)

    def drain(self):
        if self.grid.count > 1:
            block = self.buffer.at[pl.ds(0, (self.grid.count - 1) * self.band[1])]
            pltpu.make_async_remote_copy(
                src_ref=block, dst_ref=block, send_sem=self.send, recv_sem=self.recv.at[0],
                device_id=self.grid.c, device_id_type=MESH,
            ).wait_send()


class Halves:
    def __init__(self, grid, buffer, rows, send, recv):
        half = rows // 2
        self.parts = [
            Gather(grid, buffer, rows, (i * half, half), order, send.at[i], recv.at[i])
            for i, order in enumerate(((0, 1, 2, 3), (0, 2, 1, 3)))
        ]

    def start(self):
        for part in self.parts:
            part.start()

    def finish(self):
        for stage in range(4):
            for part in self.parts:
                part.finish(stage)

    def drain(self):
        for part in self.parts:
            part.drain()


def split(value):
    high = value.astype(jnp.bfloat16)
    low = (value - high.astype(jnp.float32)).astype(jnp.bfloat16)
    return high, low


def tile_of(total, want):
    while total % want:
        want //= 2
    return want


def split_rows(source, high, low):
    rows = source.shape[0]
    tile = tile_of(rows, 64)

    def step(i, carry):
        r = pl.ds(pl.multiple_of(i * tile, tile), tile)
        h, l = split(source[r, :])
        high[r, :] = h
        low[r, :] = l
        return carry

    lax.fori_loop(0, rows // tile, step, 0)


def split_beside(source, both):
    rows, width = source.shape
    tile = tile_of(rows, 128)

    def step(i, carry):
        r = pl.ds(pl.multiple_of(i * tile, tile), tile)
        h, l = split(source[r, :])
        both[r, 0:width] = h
        both[r, width : 2 * width] = l
        return carry

    lax.fori_loop(0, rows // tile, step, 0)


def product(high, low, both):
    width = both.shape[1] // 2
    wide = jnp.dot(high, both[...], preferred_element_type=jnp.float32)
    thin = jnp.dot(low, both[:, 0:width], preferred_element_type=jnp.float32)
    return wide[:, 0:width] + wide[:, width:] + thin


def by_rows(rows, want, function):
    tile = tile_of(rows, want)

    def step(i, carry):
        function(pl.ds(pl.multiple_of(i * tile, tile), tile))
        return carry

    lax.fori_loop(0, rows // tile, step, 0)


def take_rows(target, source, index, count, base=0):
    unroll = tile_of(count, 16)

    def step(i, carry):
        first = pl.multiple_of(i * unroll, unroll)
        for j in range(unroll):
            row = index[base, first + j] if len(index.shape) == 2 else index[base + first + j]
            target[pl.ds(first + j, 1), :] = source[pl.ds(row, 1), :]
        return carry

    lax.fori_loop(0, count // unroll, step, 0)


def main_kernel(
    sizes, face,
    slots, places, own_map,
    loads, start, basis, weight, map_block, schur, inverse, coarse_inv,
    solution, residual,
    full, s_high, s_low, b_high, b_low, m_high, m_low, t_high, t_low,
    c_high, c_low, coarse_own, coarse_t, map_all, map_rows, all_map, picked, field, moved, both, term_both, sol_both, coarse_rows,
    faces, arrived, term_all, sol_all,
    load_sem, map_send, map_recv, face_send, face_recv, term_send, term_recv, sol_send, sol_recv,
):
    grid = Grid(sizes)
    unknowns, cases = start.shape
    primal = basis.shape[1]
    own = coarse_t.shape[1]
    local = full.at[:, 0:cases]
    load_s = pltpu.make_async_copy(schur, full, load_sem.at[0])
    load_b = pltpu.make_async_copy(inverse, full, load_sem.at[1])
    load_s.start()
    first_own = pl.multiple_of(grid.c[2] * own, own)
    load_c = pltpu.make_async_copy(coarse_inv.at[pl.ds(first_own, own)], coarse_own, load_sem.at[2])
    load_c.start()
    map_first = pl.multiple_of(grid.linear(grid.place) * 8, 8)
    map_all[pl.ds(map_first, 8), :] = map_block[...]
    for landing in arrived:
        landing[...] = jnp.zeros_like(landing)
    grid.barrier()
    maps = Gather(grid, map_all, 8, (0, 8), (0, 1, 2, 3), map_send, map_recv)
    maps.start()
    split_rows(basis, m_high, m_low)
    for k in range(0, unknowns, primal):
        h, l = split(basis[k : k + primal, :].T)
        t_high[:, k : k + primal] = h
        t_low[:, k : k + primal] = l
    solution[...] = start[...]
    sent = []

    def face_copy(turn, d):
        axis, side = d // 2, d % 2
        target = list(grid.c)
        target[axis] = grid.c[axis] + (1 if side else -1)
        return pltpu.make_async_remote_copy(
            src_ref=faces.at[turn, pl.ds(d * face, face)],
            dst_ref=arrived[turn].at[pl.ds((d ^ 1) * face, face)],
            send_sem=face_send.at[turn, d],
            recv_sem=face_recv.at[turn, d ^ 1],
            device_id=tuple(target), device_id_type=MESH,
        )

    def exists(d):
        axis, side = d // 2, d % 2
        return grid.c[axis] < sizes[axis] - 1 if side else grid.c[axis] > 0

    def exchange_start(turn):
        for d in range(6):
            take_rows(faces.at[turn, pl.ds(d * face, face)], field, slots, face, d * face)

            @pl.when(exists(d))
            def _():
                face_copy(turn, d).start()

    def exchange_finish(turn):
        for d in range(6):

            @pl.when(exists(d))
            def _():
                block = arrived[turn].at[pl.ds(d * face, face)]
                pltpu.make_async_remote_copy(
                    src_ref=block, dst_ref=block, send_sem=face_send.at[turn, d],
                    recv_sem=face_recv.at[turn, d], device_id=grid.c, device_id_type=MESH,
                ).wait_recv()

        take_rows(moved, arrived[turn], places, unknowns)

    def exchange_drain(turn):
        for d in range(6):

            @pl.when(exists(d))
            def _():
                face_copy(turn, d).wait_send()

    gathers = []
    for iteration in range(ITERS):
        turn = 2 * iteration
        split_beside(solution, both)
        if iteration == 0:
            load_s.wait()
            split_rows(full, s_high, s_low)
            load_b.start()
            maps.finish(0)

        def stiff(r):
            field[r, :] = product(s_high[r, :], s_low[r, :], both)

        by_rows(unknowns, 256, stiff)
        if iteration == 0:
            maps.finish(1)
        exchange_start(turn)
        if iteration == 0:
            maps.finish(2)
            load_b.wait()
            split_rows(full, b_high, b_low)

            load_c.wait()
            for k in range(0, coarse_own.shape[1], primal):
                coarse_t[k : k + primal, :] = coarse_own[:, k : k + primal].T
            maps.finish(3)

            def pack(p, carry):
                map_rows[pl.ds(p, 1), :] = map_all[pl.ds(p * 8, 1), :]
                return carry

            lax.fori_loop(0, grid.count, pack, 0)
            to_scalars = pltpu.make_async_copy(map_rows, all_map, load_sem.at[3])
            to_scalars.start()
            to_scalars.wait()

            def pick(p, carry):
                take_rows(picked, coarse_t, all_map, primal, p)
                h, l = split(picked[...].T)
                k = pl.ds(pl.multiple_of(p * primal, primal), primal)
                c_high[:, k] = h
                c_low[:, k] = l
                return carry

            lax.fori_loop(0, grid.count, pick, 0)
        exchange_finish(turn)

        def settle(r):
            value = loads[r, :] - (field[r, :] + moved[r, :])
            residual[r, :] = value
            scaled = weight[r, :] * value
            h, l = split(scaled)
            both[r, 0:cases] = h
            both[r, cases : 2 * cases] = l

        by_rows(unknowns, 128, settle)
        mine = pl.multiple_of(grid.linear(grid.place) * primal, primal)
        term_all[iteration, pl.ds(mine, primal), :] = product(t_high[...], t_low[...], both)
        terms = Halves(grid, term_all.at[iteration], primal, term_send.at[iteration], term_recv.at[iteration])
        terms.start()
        gathers.append(terms)

        def invert(r):
            local[r, :] = product(b_high[r, :], b_low[r, :], both)

        by_rows(unknowns, 256, invert)
        terms.finish()
        mine = pl.multiple_of(grid.linear(grid.place) * own, own)
        coarse_tile = term_both.shape[0]
        sol_all[iteration][pl.ds(mine, own), :] = jnp.zeros((own, cases), jnp.float32)

        def coarse(i, carry):
            k = pl.ds(pl.multiple_of(i * coarse_tile, coarse_tile), coarse_tile)
            split_beside(term_all.at[iteration, k], term_both)
            sol_all[iteration][pl.ds(mine, own), :] += product(c_high[:, k], c_low[:, k], term_both)
            return carry

        lax.fori_loop(0, grid.count * primal // coarse_tile, coarse, 0)
        sols = Halves(grid, sol_all[iteration], own, sol_send.at[iteration], sol_recv.at[iteration])
        sols.start()
        sols.finish()
        gathers.append(sols)
        take_rows(coarse_rows, sol_all[iteration], own_map, primal)
        split_beside(coarse_rows, sol_both)

        def correct(r):
            field[r, :] = weight[r, :] * (local[r, :] + product(m_high[r, :], m_low[r, :], sol_both))

        by_rows(unknowns, 256, correct)
        exchange_start(turn + 1)
        exchange_finish(turn + 1)

        def advance(r):
            solution[r, :] = solution[r, :] + damping * (field[r, :] + moved[r, :])

        by_rows(unknowns, 128, advance)
    for turn in range(2 * ITERS):
        exchange_drain(turn)
    for gather in gathers + [maps]:
        gather.drain()


def places_of(slots, unknowns):
    count = slots.shape[0]
    hit = slots[:, None] == jnp.arange(unknowns, dtype=jnp.int32)[None, :]
    position = jnp.arange(count, dtype=jnp.int32)[:, None] - count
    return jnp.sum(jnp.where(hit, position, 0), axis=0) + count


def body(sizes, loads, start, schur, inv_local, basis, coarse_inv, face_index, multiplicity, primal_map):
    unknowns, cases = loads.shape[3:]
    face = face_index.shape[4]
    primal = basis.shape[4]
    count = sizes[0] * sizes[1] * sizes[2]
    total = coarse_inv.shape[1]
    own = coarse_inv.shape[0] // sizes[2]
    slots = face_index.reshape(-1)
    places = places_of(slots, unknowns)
    own_map = primal_map.reshape(-1)
    vmem = pl.BlockSpec(memory_space=pltpu.VMEM)
    smem = pl.BlockSpec(memory_space=pltpu.SMEM)
    anywhere = pl.BlockSpec(memory_space=pl.ANY)
    dma = pltpu.SemaphoreType.DMA
    weight = jnp.broadcast_to(
        1.0 / multiplicity.reshape(unknowns, 1).astype(jnp.float32), (unknowns, cases)
    )
    modes = basis.reshape(unknowns, primal)
    f32, bf16 = jnp.float32, jnp.bfloat16
    turns = 2 * ITERS
    coarse_tile = tile_of(count * primal, 1024)
    vec = pltpu.VMEM((unknowns, cases), f32)
    out = jax.ShapeDtypeStruct((unknowns, cases), f32)
    solution, residual = pl.pallas_call(
        functools.partial(main_kernel, sizes, face),
        out_shape=(out, out),
        in_specs=[smem] * 3 + [vmem] * 5 + [anywhere] * 3,
        out_specs=(vmem, vmem),
        scratch_shapes=[
            pltpu.VMEM((unknowns, unknowns), f32),
            pltpu.VMEM((unknowns, unknowns), bf16),
            pltpu.VMEM((unknowns, unknowns), bf16),
            pltpu.VMEM((unknowns, unknowns), bf16),
            pltpu.VMEM((unknowns, unknowns), bf16),
            pltpu.VMEM((unknowns, primal), bf16),
            pltpu.VMEM((unknowns, primal), bf16),
            pltpu.VMEM((primal, unknowns), bf16),
            pltpu.VMEM((primal, unknowns), bf16),
            pltpu.VMEM((own, count * primal), bf16),
            pltpu.VMEM((own, count * primal), bf16),
            pltpu.VMEM((own, total), f32),
            pltpu.VMEM((total, own), f32),
            pltpu.VMEM((count * 8, primal), jnp.int32),
            pltpu.VMEM((count, primal), jnp.int32),
            pltpu.SMEM((count, primal), jnp.int32),
            pltpu.VMEM((primal, own), f32),
            vec, vec,
            pltpu.VMEM((unknowns, 2 * cases), bf16),
            pltpu.VMEM((coarse_tile, 2 * cases), bf16),
            pltpu.VMEM((primal, 2 * cases), bf16),
            pltpu.VMEM((primal, cases), f32),
            pltpu.VMEM((turns, 6 * face, cases), f32),
            [pltpu.VMEM((6 * face + 8, cases), f32) for _ in range(turns)],
            pltpu.VMEM((ITERS, count * primal, cases), f32),
            [pltpu.VMEM((total, cases), f32) for _ in range(ITERS)],
            dma((4,)),
            dma(()), dma((count,)),
            dma((turns, 6)), dma((turns, 6)),
            dma((ITERS, 2)), dma((ITERS, 2, count)),
            dma((ITERS, 2)), dma((ITERS, 2, count)),
        ],
        compiler_params=pltpu.CompilerParams(
            collective_id=1, has_side_effects=True, vmem_limit_bytes=67043328
        ),
    )(
        slots, places, own_map,
        loads.reshape(unknowns, cases), start.reshape(unknowns, cases),
        modes, weight, jnp.broadcast_to(own_map[None, :], (8, primal)),
        schur.reshape(unknowns, unknowns), inv_local.reshape(unknowns, unknowns), coarse_inv,
    )
    return (solution.reshape(loads.shape), residual.reshape(loads.shape))


def solution(mesh):
    sizes = tuple(mesh.shape[a] for a in AXES)
    field = P("gx", "gy", "gz", None, None)
    placed = (field,) * 5 + (P(("gx", "gy"), None), field, P("gx", "gy", "gz", None), P("gx", "gy", "gz", None))
    return jax.shard_map(
        functools.partial(body, sizes),
        mesh=mesh,
        in_specs=placed,
        out_specs=(field, field),
        check_vma=False,
    )
```
